32 devices in a mesh: prow: 8 (over y, x, core), pcol: 4 (over z).
Axes of the slice: x: 2, y: 2, z: 4, core: 2. Of those that a mesh axis runs over, the one named last changes fastest.
Arguments:
- inverse: bfloat16 [4, 4096, 8, 2048], P(None, 'prow', None, 'pcol'), may hold values from -6 to 6
- panel: bfloat16 [2, 4, 4096, 256], P(None, None, 'prow'), may hold values from -0.09375 to 0.09375
- structure: int32 [2, 8], replicated, may hold values from 0 to 31, as said below
- diag_inverse: float32 [2, 256, 256], replicated, may hold values from -6 to 6
Outputs:
- off_diag: bfloat16 [2, 4, 4096, 256], P(None, None, ('prow', 'pcol'))
- diag_block: float32 [2, 256, 256], replicated
The draws below stay inside these ranges and needn't reach their ends.
Inputs may be any that keep to these rules, and one draw needn't show every extreme that they name: `structure`: each row lists 8 distinct block indices in increasing order, exactly one of them congruent to p modulo 8 for every p, and always includes the last ancestor block 31.
All inputs are finite; a program needn't handle non-finite values.
Results may differ from the reference program's by a relative error of at most 0.0022.
Values may be sent and summed in bfloat16 or wider, within the bound.
A program may use at most 128 MiB of HBM per device.

```python
import jax
import jax.numpy as jnp

BLK = 512
W = 256
NODES = 2
BR_DEV = 4
BC_DEV = 8
SEL = 8
N_PROW = 8
N_PCOL = 4


def draw_structure(key, part):
    listed = []
    for supernode in range(NODES):
        subkey = jax.random.fold_in(key, 17 + supernode)
        offsets = jax.random.randint(subkey, (SEL,), 0, BR_DEV).astype(jnp.int32)
        offsets = offsets.at[SEL - 1].set(BR_DEV - 1)
        indices = offsets * SEL + jnp.arange(SEL, dtype=jnp.int32)
        listed.append(jnp.sort(indices))
    return jnp.stack(listed).astype(jnp.int32)


def block_levels(rng, extent, cuts, smallest, largest):
    level = 1.0
    for position, shards_of in cuts:
        heights = jax.random.uniform(jax.random.fold_in(jax.random.fold_in(rng, 6), position), (shards_of,), jnp.float32, smallest / len(cuts), largest / len(cuts))
        level = level * jnp.repeat(jnp.exp(heights), extent[position] // shards_of).reshape((-1,) + (1,) * (len(extent) - 1 - position))
    return level


def bell_draw(stream_key, extent, spread, bound, cuts=(), kind=jnp.bfloat16):
    array = spread * jax.random.normal(stream_key, extent, jnp.float32)
    if cuts:
        array = array * block_levels(stream_key, extent, cuts, -0.22, 0.18)
    return jnp.clip(array, -bound, bound).astype(kind)


def setup_inputs(seed: int = 0) -> dict:
    key_of = jax.random.split(jax.random.key(seed), 5)
    inverse = bell_draw(key_of[0], (BR_DEV, N_PROW * BLK, BC_DEV, N_PCOL * BLK), 1.0, 6.0, ((1, 8), (3, 4)))
    panel = bell_draw(key_of[1], (NODES, BR_DEV, N_PROW * BLK, W), (SEL * BLK) ** -0.5, 0.09375, ((2, 8),))
    structure = draw_structure(jax.random.fold_in(key_of[4], 71), 0)
    diag_inverse = bell_draw(key_of[3], (NODES, W, W), 1.0, 6.0, (), jnp.float32)
    return {"inverse": inverse, "panel": panel, "structure": structure, "diag_inverse": diag_inverse}


def reference(inverse, panel, structure, diag_inverse):
    total_blocks = BR_DEV * N_PROW
    blocks = inverse.reshape(total_blocks, BLK, total_blocks, BLK)
    pieces = []
    products = []
    for supernode in range(NODES):
        chosen = structure[supernode]
        factor_blocks = panel[supernode].reshape(total_blocks, BLK, W)
        factor_rows = jnp.take(factor_blocks, chosen, axis=0).reshape(SEL * BLK, W)
        picked = jnp.take(jnp.take(blocks, chosen, axis=0), chosen, axis=2).reshape(SEL * BLK, SEL * BLK)
        result = (-jnp.dot(picked, factor_rows, preferred_element_type=jnp.float32)).astype(jnp.bfloat16)
        placed = jnp.zeros((total_blocks, BLK, W), jnp.bfloat16).at[chosen].set(result.reshape(SEL, BLK, W))
        pieces.append(placed.reshape(BR_DEV, N_PROW * BLK, W))
        products.append(jnp.dot(factor_rows.T, result, preferred_element_type=jnp.float32))
    return jnp.stack(pieces), diag_inverse - jnp.stack(products)
```

```python
import functools

import jax
import jax.numpy as jnp
from jax import lax
from jax.experimental import pallas as pl
from jax.experimental.pallas import tpu as pltpu
from jax.sharding import PartitionSpec as P

MESH = pl.DeviceIdType.MESH
CHUNKS = 2


def remote(src, dst, send, recv, p, q):
    return pltpu.make_async_remote_copy(
        src_ref=src, dst_ref=dst, send_sem=send, recv_sem=recv, device_id=(p, q), device_id_type=MESH
    )


def fused(
    n_rows, n_cols, a_ref, l_ref, d_ref, y_ref, g_ref,
    l_buf, part, right_buf, left_buf, term, plane_buf, col_buf, gath,
    l_send, l_recv, r_send, r_recv, f_send, f_recv, p_send, p_recv, c_send, c_recv, g_send, g_recv,
):
    p = lax.axis_index("prow")
    q = lax.axis_index("pcol")
    nodes, ratio, block, width = l_buf.shape
    piece = block // n_cols
    seg = width // n_rows
    chunk = block // CHUNKS
    hi = p // n_cols
    lo = p % n_cols
    t = jnp.int32(0)
    bit = 1
    while bit < n_cols:
        t = t + bit * (((lo // bit) + (q // bit)) % 2)
        bit *= 2
    pair = p + 1 - 2 * (p % 2)

    def same_hi(t2):
        lo2 = jnp.int32(0)
        b = 1
        while b < n_cols:
            lo2 = lo2 + b * (((t2 // b) + (q // b)) % 2)
            b *= 2
        return hi * n_cols + lo2

    barrier = pltpu.get_barrier_semaphore()
    for k in range(1, n_rows):
        pl.semaphore_signal(barrier, inc=1, device_id=((p + k) % n_rows, q), device_id_type=MESH)
    for k in range(1, n_cols):
        pl.semaphore_signal(barrier, inc=1, device_id=(p, (q + k) % n_cols), device_id_type=MESH)
    pl.semaphore_wait(barrier, n_rows + n_cols - 2)

    def rows(c):
        return pl.ds(c * chunk, chunk)

    def l_slot(s, h, c):
        return l_buf.at[s, h, rows(c)]

    def to_peer_hi(s, c, k, src):
        return remote(src, l_slot(s, hi, c), l_send.at[s, c, k - 1], l_recv.at[s, hi, c],
                      (p + k * n_cols) % n_rows, q)

    def to_x(s, c, j, src):
        return remote(src, l_slot(s, hi, c), l_send.at[s, c, ratio - 1 + j - 1], l_recv.at[s, hi, c],
                      same_hi(2 * j), q)

    def to_pair(s, c, k, src):
        h = (hi + k) % ratio
        return remote(src, l_slot(s, h, c), l_send.at[s, c, ratio - 1 + n_cols // 2 - 1 + k],
                      l_recv.at[s, h, c], pair, q)

    def l_arrived(s, c, h):
        remote(l_slot(s, h, c), l_slot(s, h, c), l_send.at[s, c, 0], l_recv.at[s, h, c], pair, q).wait_recv()

    owner = t == 0
    even = t % 2 == 0

    @pl.when(owner)
    def _():
        for s in range(nodes):
            for c in range(CHUNKS):
                src = l_ref.at[s, rows(c)]
                for j in range(1, n_cols // 2):
                    to_x(s, c, j, src).start()
                for k in range(1, ratio):
                    to_peer_hi(s, c, k, src).start()
                to_pair(s, c, 0, src).start()
        for s in range(nodes):
            l_buf[s, hi] = l_ref[s]

    def receive_blocks(s):
        for c in range(CHUNKS):
            @pl.when(jnp.logical_not(owner))
            def _():
                l_arrived(s, c, hi)

            @pl.when(jnp.logical_and(even, jnp.logical_not(owner)))
            def _():
                for k in range(1, ratio):
                    to_peer_hi(s, c, k, l_slot(s, hi, c)).start()
                to_pair(s, c, 0, l_slot(s, hi, c)).start()

            for k in range(1, ratio):
                l_arrived(s, c, (hi + k) % ratio)

                @pl.when(even)
                def _():
                    to_pair(s, c, k, l_slot(s, (hi + k) % ratio, c)).start()

    def drain_blocks(s):
        for c in range(CHUNKS):
            @pl.when(even)
            def _():
                src = l_slot(s, hi, c)
                for k in range(1, ratio):
                    to_peer_hi(s, c, k, src).wait_send()
                for k in range(ratio):
                    to_pair(s, c, k, src).wait_send()

            @pl.when(owner)
            def _():
                for j in range(1, n_cols // 2):
                    to_x(s, c, j, l_slot(s, hi, c)).wait_send()

    def multiply(s):
        total = jnp.dot(a_ref[s, 0], l_buf[s, 0], preferred_element_type=jnp.float32)
        for h in range(1, ratio):
            total += jnp.dot(a_ref[s, h], l_buf[s, h], preferred_element_type=jnp.float32)
        for d in range(n_cols):
            part[s, d] = total[d * piece:(d + 1) * piece]

    def right_copy(s, d, src):
        return remote(src, right_buf.at[s, d], r_send.at[s, d], r_recv.at[s, d], p, (q + 1) % n_cols)

    def left_copy(s, d, src):
        return remote(src, left_buf.at[s, d], f_send.at[s, d], f_recv.at[s, d], p, (q + n_cols - 1) % n_cols)

    def line_start(s):
        @pl.when(q == 0)
        def _():
            for d in range(n_cols - 1, 0, -1):
                right_copy(s, d, part.at[s, d]).start()

        @pl.when(q == n_cols - 1)
        def _():
            for d in range(n_cols - 1):
                left_copy(s, d, part.at[s, d]).start()

    def line_relay(s):
        for i in range(n_cols - 2):
            d = n_cols - 1 - i

            @pl.when(jnp.logical_and(q > 0, q < d))
            def _():
                right_copy(s, d, right_buf.at[s, d]).wait_recv()
                right_buf[s, d] = right_buf[s, d] + part[s, d]
                right_copy(s, d, right_buf.at[s, d]).start()

            e = i

            @pl.when(jnp.logical_and(q < n_cols - 1, q > e))
            def _():
                left_copy(s, e, left_buf.at[s, e]).wait_recv()
                left_buf[s, e] = left_buf[s, e] + part[s, e]
                left_copy(s, e, left_buf.at[s, e]).start()

    def line_finish(s):
        @pl.when(q > 0)
        def _():
            right_copy(s, q, right_buf.at[s, q]).wait_recv()
            part[s, q] = part[s, q] + right_buf[s, q]

        @pl.when(q < n_cols - 1)
        def _():
            left_copy(s, q, left_buf.at[s, q]).wait_recv()
            part[s, q] = part[s, q] + left_buf[s, q]

        rounded = (-part[s, q]).astype(jnp.bfloat16)
        y_ref[s] = rounded
        factor = l_ref[s, pl.ds(pl.multiple_of(q * piece, piece), piece)]
        product = lax.dot_general(
            factor, rounded, (((0,), (0,)), ((), ())), preferred_element_type=jnp.float32
        )
        for k in range(n_rows):
            term[s, k] = product[k * seg:(k + 1) * seg]

    def line_drain(s):
        for d in range(n_cols):
            @pl.when(q < d)
            def _():
                right_copy(s, d, part.at[s, d]).wait_send()

            @pl.when(q > d)
            def _():
                left_copy(s, d, part.at[s, d]).wait_send()

    def plane_copy(s, k):
        to = (p + k) % n_rows
        return remote(term.at[s, to], plane_buf.at[s, n_rows - k], p_send.at[s, k], p_recv.at[s, n_rows - k], to, q)

    def plane_wait(s, k):
        remote(term.at[s, 0], plane_buf.at[s, k], p_send.at[s, k], p_recv.at[s, k], pair, q).wait_recv()

    def col_copy(s, k):
        to = (q + k) % n_cols
        return remote(col_buf.at[s, q], col_buf.at[s, q], c_send.at[s, k], c_recv.at[s, n_cols - k], p, to)

    def col_wait(s, k):
        src = (q + k) % n_cols
        remote(col_buf.at[s, src], col_buf.at[s, src], c_send.at[s, k], c_recv.at[s, k], pair, q).wait_recv()

    def gath_copy(s, k):
        to = (p + k) % n_rows
        return remote(gath.at[s, p], gath.at[s, p], g_send.at[s, k], g_recv.at[s, n_rows - k], to, q)

    def gath_wait(s, k):
        src = (p + k) % n_rows
        remote(gath.at[s, src], gath.at[s, src], g_send.at[s, k], g_recv.at[s, k], pair, q).wait_recv()

    def plane_start(s):
        for k in range(1, n_rows):
            plane_copy(s, k).start()

    def col_start(s):
        total = term[s, p]
        for k in range(1, n_rows):
            plane_wait(s, k)
            total = total + plane_buf[s, k]
        col_buf[s, q] = total
        for k in range(1, n_cols):
            col_copy(s, k).start()

    def gath_start(s):
        for k in range(1, n_cols):
            col_wait(s, k)
        total = col_buf[s, 0]
        for k in range(1, n_cols):
            total = total + col_buf[s, k]
        gath[s, p] = d_ref[s, pl.ds(pl.multiple_of(p * seg, seg), seg)] - total
        for k in range(1, n_rows):
            gath_copy(s, k).start()

    for s in range(nodes):
        receive_blocks(s)
        multiply(s)
        line_start(s)
    for s in range(nodes):
        line_relay(s)
        line_finish(s)
        plane_start(s)
    for s in range(nodes):
        col_start(s)
    for s in range(nodes):
        gath_start(s)
    for s in range(nodes):
        drain_blocks(s)
        line_drain(s)
        for k in range(1, n_rows):
            plane_copy(s, k).wait_send()
        for k in range(1, n_cols):
            col_copy(s, k).wait_send()
    for s in range(nodes):
        for k in range(1, n_rows):
            gath_wait(s, k)
        for k in range(n_rows):
            g_ref[s, k * seg:(k + 1) * seg] = gath[s, k]
    for s in range(nodes):
        for k in range(1, n_rows):
            gath_copy(s, k).wait_send()


def on_device(inverse, panel, structure, diag_inverse):
    n_rows = lax.axis_size("prow")
    n_cols = lax.axis_size("pcol")
    p = lax.axis_index("prow")
    q = lax.axis_index("pcol")
    rows_local, block, cols_local, _ = inverse.shape
    nodes, _, _, width = panel.shape
    ratio = n_rows // n_cols
    piece = block // n_cols
    seg = width // n_rows

    picked_a = []
    picked_l = []
    row_picks = []
    for s in range(nodes):
        chosen = structure[s]
        row = jnp.sum(jnp.where(chosen % n_rows == p, chosen // n_rows, 0))
        row_picks.append(row)
        picked_l.append(lax.dynamic_slice(panel, (s, row, 0, 0), (1, 1, block, width))[0, 0])
        for h in range(ratio):
            col = jnp.sum(jnp.where(chosen % n_rows == h * n_cols + q, chosen // n_cols, 0))
            picked_a.append(
                lax.dynamic_slice(inverse, (row, 0, col, 0), (1, block, 1, block))[0, :, 0, :]
            )
    a_sel = jnp.stack(picked_a).reshape(nodes, ratio, block, block)
    l_sel = jnp.stack(picked_l)

    f32 = jnp.float32
    dma = pltpu.SemaphoreType.DMA
    sends = ratio - 1 + n_cols // 2 - 1 + ratio
    vmem = pl.BlockSpec(memory_space=pltpu.VMEM)
    pieces, diagonal = pl.pallas_call(
        functools.partial(fused, n_rows, n_cols),
        out_shape=(
            jax.ShapeDtypeStruct((nodes, piece, width), jnp.bfloat16),
            jax.ShapeDtypeStruct((nodes, width, width), f32),
        ),
        in_specs=[vmem] * 3,
        out_specs=(vmem, vmem),
        scratch_shapes=[
            pltpu.VMEM((nodes, ratio, block, width), jnp.bfloat16),
            pltpu.VMEM((nodes, n_cols, piece, width), f32),
            pltpu.VMEM((nodes, n_cols, piece, width), f32),
            pltpu.VMEM((nodes, n_cols, piece, width), f32),
            pltpu.VMEM((nodes, n_rows, seg, width), f32),
            pltpu.VMEM((nodes, n_rows, seg, width), f32),
            pltpu.VMEM((nodes, n_cols, seg, width), f32),
            pltpu.VMEM((nodes, n_rows, seg, width), f32),
            dma((nodes, CHUNKS, sends)), dma((nodes, ratio, CHUNKS)),
            dma((nodes, n_cols)), dma((nodes, n_cols)),
            dma((nodes, n_cols)), dma((nodes, n_cols)),
            dma((nodes, n_rows)), dma((nodes, n_rows)),
            dma((nodes, n_cols)), dma((nodes, n_cols)),
            dma((nodes, n_rows)), dma((nodes, n_rows)),
        ],
        compiler_params=pltpu.CompilerParams(
            collective_id=0, has_side_effects=True, vmem_limit_bytes=40 * 1024 * 1024
        ),
        name="selected_inverse",
    )(a_sel, l_sel, diag_inverse)

    local = jnp.arange(rows_local, dtype=jnp.int32)
    mask = jnp.stack(row_picks)[:, None] == local[None, :]
    off_diag = jnp.where(mask[:, :, None, None], pieces[:, None], jnp.zeros((), jnp.bfloat16))
    return off_diag, diagonal


def solution(mesh):
    placed = (P(None, "prow", None, "pcol"), P(None, None, "prow", None), P(), P())
    return jax.shard_map(
        on_device,
        mesh=mesh,
        in_specs=placed,
        out_specs=(P(None, None, ("prow", "pcol"), None), P()),
        check_vma=False,
    )
```

```python
import functools

import jax
import jax.numpy as jnp
from jax import lax
from jax.experimental import pallas as pl
from jax.experimental.pallas import tpu as pltpu
from jax.sharding import PartitionSpec as P

MESH = pl.DeviceIdType.MESH
CHUNKS = 2
STRIPS = 4


def remote(src, dst, send, recv, p, q):
    return pltpu.make_async_remote_copy(
        src_ref=src, dst_ref=dst, send_sem=send, recv_sem=recv, device_id=(p, q), device_id_type=MESH
    )


def fused(
    n_rows, n_cols, a_ref, l_ref, d_ref, y_ref, g_ref,
    l_buf, part, right_buf, left_buf, term, plane_buf, col_buf, gath,
    l_send, l_recv, r_send, r_recv, f_send, f_recv, p_send, p_recv, c_send, c_recv, g_send, g_recv,
):
    p = lax.axis_index("prow")
    q = lax.axis_index("pcol")
    nodes, ratio, block, width = l_buf.shape
    piece = block // n_cols
    seg = width // n_rows
    chunk = block // CHUNKS
    hi = p // n_cols
    lo = p % n_cols
    t = jnp.int32(0)
    bit = 1
    while bit < n_cols:
        t = t + bit * (((lo // bit) + (q // bit)) % 2)
        bit *= 2
    pair = p + 1 - 2 * (p % 2)

    def same_hi(t2):
        lo2 = jnp.int32(0)
        b = 1
        while b < n_cols:
            lo2 = lo2 + b * (((t2 // b) + (q // b)) % 2)
            b *= 2
        return hi * n_cols + lo2

    barrier = pltpu.get_barrier_semaphore()
    for k in range(1, n_rows):
        pl.semaphore_signal(barrier, inc=1, device_id=((p + k) % n_rows, q), device_id_type=MESH)
    for k in range(1, n_cols):
        pl.semaphore_signal(barrier, inc=1, device_id=(p, (q + k) % n_cols), device_id_type=MESH)
    pl.semaphore_wait(barrier, n_rows + n_cols - 2)

    def rows(c):
        return pl.ds(c * chunk, chunk)

    def l_slot(s, h, c):
        return l_buf.at[s, h, rows(c)]

    def to_peer_hi(s, c, k, src):
        return remote(src, l_slot(s, hi, c), l_send.at[s, c, k - 1], l_recv.at[s, hi, c],
                      (p + k * n_cols) % n_rows, q)

    def to_x(s, c, j, src):
        return remote(src, l_slot(s, hi, c), l_send.at[s, c, ratio - 1 + j - 1], l_recv.at[s, hi, c],
                      same_hi(2 * j), q)

    def to_pair(s, c, k, src):
        h = (hi + k) % ratio
        return remote(src, l_slot(s, h, c), l_send.at[s, c, ratio - 1 + n_cols // 2 - 1 + k],
                      l_recv.at[s, h, c], pair, q)

    def l_arrived(s, c, h):
        remote(l_slot(s, h, c), l_slot(s, h, c), l_send.at[s, c, 0], l_recv.at[s, h, c], pair, q).wait_recv()

    owner = t == 0
    even = t % 2 == 0

    @pl.when(owner)
    def _():
        for s in range(nodes):
            for c in range(CHUNKS):
                src = l_ref.at[s, rows(c)]
                for j in range(1, n_cols // 2):
                    to_x(s, c, j, src).start()
                for k in range(1, ratio):
                    to_peer_hi(s, c, k, src).start()
                to_pair(s, c, 0, src).start()
        for s in range(nodes):
            l_buf[s, hi] = l_ref[s]

    def receive_blocks(s):
        for c in range(CHUNKS):
            @pl.when(jnp.logical_not(owner))
            def _():
                l_arrived(s, c, hi)

            @pl.when(jnp.logical_and(even, jnp.logical_not(owner)))
            def _():
                for k in range(1, ratio):
                    to_peer_hi(s, c, k, l_slot(s, hi, c)).start()
                to_pair(s, c, 0, l_slot(s, hi, c)).start()

            for k in range(1, ratio):
                l_arrived(s, c, (hi + k) % ratio)

                @pl.when(even)
                def _():
                    to_pair(s, c, k, l_slot(s, (hi + k) % ratio, c)).start()

    def drain_blocks(s):
        for c in range(CHUNKS):
            @pl.when(even)
            def _():
                src = l_slot(s, hi, c)
                for k in range(1, ratio):
                    to_peer_hi(s, c, k, src).wait_send()
                for k in range(ratio):
                    to_pair(s, c, k, src).wait_send()

            @pl.when(owner)
            def _():
                for j in range(1, n_cols // 2):
                    to_x(s, c, j, l_slot(s, hi, c)).wait_send()

    def multiply(s):
        total = jnp.dot(a_ref[s, 0], l_buf[s, 0], preferred_element_type=jnp.float32)
        for h in range(1, ratio):
            total += jnp.dot(a_ref[s, h], l_buf[s, h], preferred_element_type=jnp.float32)
        for d in range(n_cols):
            part[s, d] = total[d * piece:(d + 1) * piece]

    def right_copy(s, d, src):
        return remote(src, right_buf.at[s, d], r_send.at[s, d], r_recv.at[s, d], p, (q + 1) % n_cols)

    def left_copy(s, d, src):
        return remote(src, left_buf.at[s, d], f_send.at[s, d], f_recv.at[s, d], p, (q + n_cols - 1) % n_cols)

    def line_start(s):
        @pl.when(q == 0)
        def _():
            for d in range(n_cols - 1, 0, -1):
                right_copy(s, d, part.at[s, d]).start()

        @pl.when(q == n_cols - 1)
        def _():
            for d in range(n_cols - 1):
                left_copy(s, d, part.at[s, d]).start()

    def line_relay(s):
        for i in range(n_cols - 2):
            d = n_cols - 1 - i

            @pl.when(jnp.logical_and(q > 0, q < d))
            def _():
                right_copy(s, d, right_buf.at[s, d]).wait_recv()
                right_buf[s, d] = right_buf[s, d] + part[s, d]
                right_copy(s, d, right_buf.at[s, d]).start()

            e = i

            @pl.when(jnp.logical_and(q < n_cols - 1, q > e))
            def _():
                left_copy(s, e, left_buf.at[s, e]).wait_recv()
                left_buf[s, e] = left_buf[s, e] + part[s, e]
                left_copy(s, e, left_buf.at[s, e]).start()

    def line_finish(s):
        @pl.when(q > 0)
        def _():
            right_copy(s, q, right_buf.at[s, q]).wait_recv()
            part[s, q] = part[s, q] + right_buf[s, q]

        @pl.when(q < n_cols - 1)
        def _():
            left_copy(s, q, left_buf.at[s, q]).wait_recv()
            part[s, q] = part[s, q] + left_buf[s, q]

        rounded = (-part[s, q]).astype(jnp.bfloat16)
        y_ref[s] = rounded
        factor = l_ref[s, pl.ds(pl.multiple_of(q * piece, piece), piece)]
        product = lax.dot_general(
            factor, rounded, (((0,), (0,)), ((), ())), preferred_element_type=jnp.float32
        )
        for k in range(n_rows):
            term[s, k] = product[k * seg:(k + 1) * seg]

    def line_drain(s):
        for d in range(n_cols):
            @pl.when(q < d)
            def _():
                right_copy(s, d, part.at[s, d]).wait_send()

            @pl.when(q > d)
            def _():
                left_copy(s, d, part.at[s, d]).wait_send()

    def plane_copy(s, k):
        to = (p + k) % n_rows
        return remote(term.at[s, to], plane_buf.at[s, n_rows - k], p_send.at[s, k], p_recv.at[s, n_rows - k], to, q)

    def plane_wait(s, k):
        remote(term.at[s, 0], plane_buf.at[s, k], p_send.at[s, k], p_recv.at[s, k], pair, q).wait_recv()

    def col_copy(s, k):
        to = (q + k) % n_cols
        return remote(col_buf.at[s, q], col_buf.at[s, q], c_send.at[s, k], c_recv.at[s, n_cols - k], p, to)

    def col_wait(s, k):
        src = (q + k) % n_cols
        remote(col_buf.at[s, src], col_buf.at[s, src], c_send.at[s, k], c_recv.at[s, k], pair, q).wait_recv()

    def gath_copy(s, k):
        to = (p + k) % n_rows
        return remote(gath.at[s, p], gath.at[s, p], g_send.at[s, k], g_recv.at[s, n_rows - k], to, q)

    def gath_wait(s, k):
        src = (p + k) % n_rows
        remote(gath.at[s, src], gath.at[s, src], g_send.at[s, k], g_recv.at[s, k], pair, q).wait_recv()

    def plane_start(s):
        for k in range(1, n_rows):
            plane_copy(s, k).start()

    def col_start(s):
        total = term[s, p]
        for k in range(1, n_rows):
            plane_wait(s, k)
            total = total + plane_buf[s, k]
        col_buf[s, q] = total
        for k in range(1, n_cols):
            col_copy(s, k).start()

    def gath_start(s):
        for k in range(1, n_cols):
            col_wait(s, k)
        total = col_buf[s, 0]
        for k in range(1, n_cols):
            total = total + col_buf[s, k]
        gath[s, p] = d_ref[s, pl.ds(pl.multiple_of(p * seg, seg), seg)] - total
        for k in range(1, n_rows):
            gath_copy(s, k).start()

    for s in range(nodes):
        receive_blocks(s)
        multiply(s)
        line_start(s)
    for s in range(nodes):
        line_relay(s)
        line_finish(s)
        plane_start(s)
    for s in range(nodes):
        col_start(s)
    for s in range(nodes):
        gath_start(s)
    for s in range(nodes):
        drain_blocks(s)
        line_drain(s)
        for k in range(1, n_rows):
            plane_copy(s, k).wait_send()
        for k in range(1, n_cols):
            col_copy(s, k).wait_send()
    for s in range(nodes):
        for k in range(1, n_rows):
            gath_wait(s, k)
        for k in range(n_rows):
            g_ref[s, k * seg:(k + 1) * seg] = gath[s, k]
    for s in range(nodes):
        for k in range(1, n_rows):
            gath_copy(s, k).wait_send()


def pick(
    n_rows, n_cols, structure_ref, inverse_ref, panel_ref, a_ref, l_ref, mask_ref, raw, wide, a_sem, l_sem
):
    p = lax.axis_index("prow")
    q = lax.axis_index("pcol")
    nodes, ratio, block, _ = a_ref.shape
    _, strips, strip, cols_local, _ = raw.shape
    rows_local = inverse_ref.shape[0]
    listed = structure_ref.shape[1]

    def find(s, residue, divisor):
        found = jnp.int32(0)
        for i in range(listed):
            value = structure_ref[s, i]
            found = found + jnp.where(value % n_rows == residue, value // divisor, 0)
        return found

    copies = []
    for s in range(nodes):
        row = find(s, p, n_rows)
        factor = pltpu.make_async_copy(panel_ref.at[s, row], l_ref.at[s], l_sem.at[s])
        factor.start()
        copies.append(factor)
        for k in range(strips):
            pltpu.make_async_copy(
                inverse_ref.at[row, pl.ds(k * strip, strip)], raw.at[s, k], a_sem.at[s, k]
            ).start()
        for r in range(rows_local):
            mask_ref[s, r] = jnp.where(row == r, 1, 0).astype(jnp.int32)
    for s in range(nodes):
        cols = [find(s, h * n_cols + q, n_cols) for h in range(ratio)]
        for k in range(strips):
            pltpu.make_async_copy(
                inverse_ref.at[0, pl.ds(k * strip, strip)], raw.at[s, k], a_sem.at[s, k]
            ).wait()
            slot = k % 2
            for b in range(block // 128):
                lanes = raw[s, k, :, :, b * 128:(b + 1) * 128].astype(jnp.float32)
                wide[slot, b] = lanes.reshape(strip * cols_local, 128)
            for h in range(ratio):
                for b in range(block // 128):
                    a_ref[s, h, k * strip:(k + 1) * strip, b * 128:(b + 1) * 128] = wide[
                        slot, b, pl.ds(cols[h], strip, stride=cols_local)
                    ].astype(jnp.bfloat16)
    for factor in copies:
        factor.wait()


def on_device(inverse, panel, structure, diag_inverse):
    n_rows = lax.axis_size("prow")
    n_cols = lax.axis_size("pcol")
    rows_local, block, cols_local, _ = inverse.shape
    nodes, _, _, width = panel.shape
    ratio = n_rows // n_cols
    piece = block // n_cols
    seg = width // n_rows
    strip = block // STRIPS

    vmem = pl.BlockSpec(memory_space=pltpu.VMEM)
    smem = pl.BlockSpec(memory_space=pltpu.SMEM)
    hbm = pl.BlockSpec(memory_space=pltpu.HBM)
    a_sel, l_sel, mask = pl.pallas_call(
        functools.partial(pick, n_rows, n_cols),
        out_shape=(
            jax.ShapeDtypeStruct((nodes, ratio, block, block), jnp.bfloat16),
            jax.ShapeDtypeStruct((nodes, block, width), jnp.bfloat16),
            jax.ShapeDtypeStruct((nodes, rows_local), jnp.int32),
        ),
        in_specs=[smem, hbm, hbm],
        out_specs=(vmem, vmem, smem),
        scratch_shapes=[
            pltpu.VMEM((nodes, STRIPS, strip, cols_local, block), jnp.bfloat16),
            pltpu.VMEM((2, block // 128, strip * cols_local, 128), jnp.float32),
            pltpu.SemaphoreType.DMA((nodes, STRIPS)),
            pltpu.SemaphoreType.DMA((nodes,)),
        ],
        compiler_params=pltpu.CompilerParams(vmem_limit_bytes=50 * 1024 * 1024),
        name="pick_blocks",
    )(structure, inverse, panel)

    f32 = jnp.float32
    dma = pltpu.SemaphoreType.DMA
    sends = ratio - 1 + n_cols // 2 - 1 + ratio
    pieces, diagonal = pl.pallas_call(
        functools.partial(fused, n_rows, n_cols),
        out_shape=(
            jax.ShapeDtypeStruct((nodes, piece, width), jnp.bfloat16),
            jax.ShapeDtypeStruct((nodes, width, width), f32),
        ),
        in_specs=[vmem] * 3,
        out_specs=(vmem, vmem),
        scratch_shapes=[
            pltpu.VMEM((nodes, ratio, block, width), jnp.bfloat16),
            pltpu.VMEM((nodes, n_cols, piece, width), f32),
            pltpu.VMEM((nodes, n_cols, piece, width), f32),
            pltpu.VMEM((nodes, n_cols, piece, width), f32),
            pltpu.VMEM((nodes, n_rows, seg, width), f32),
            pltpu.VMEM((nodes, n_rows, seg, width), f32),
            pltpu.VMEM((nodes, n_cols, seg, width), f32),
            pltpu.VMEM((nodes, n_rows, seg, width), f32),
            dma((nodes, CHUNKS, sends)), dma((nodes, ratio, CHUNKS)),
            dma((nodes, n_cols)), dma((nodes, n_cols)),
            dma((nodes, n_cols)), dma((nodes, n_cols)),
            dma((nodes, n_rows)), dma((nodes, n_rows)),
            dma((nodes, n_cols)), dma((nodes, n_cols)),
            dma((nodes, n_rows)), dma((nodes, n_rows)),
        ],
        compiler_params=pltpu.CompilerParams(
            collective_id=0, has_side_effects=True, vmem_limit_bytes=40 * 1024 * 1024
        ),
        name="selected_inverse",
    )(a_sel, l_sel, diag_inverse)

    off_diag = jnp.where(mask[:, :, None, None] > 0, pieces[:, None], jnp.zeros((), jnp.bfloat16))
    return off_diag, diagonal


def solution(mesh):
    placed = (P(None, "prow", None, "pcol"), P(None, None, "prow", None), P(), P())
    return jax.shard_map(
        on_device,
        mesh=mesh,
        in_specs=placed,
        out_specs=(P(None, None, ("prow", "pcol"), None), P()),
        check_vma=False,
    )
```

```python
import functools

import jax
import jax.numpy as jnp
from jax import lax
from jax.experimental import pallas as pl
from jax.experimental.pallas import tpu as pltpu
from jax.sharding import PartitionSpec as P

MESH = pl.DeviceIdType.MESH
SUB = 2
STRIPS = 4


def remote(src, dst, send, recv, p, q):
    return pltpu.make_async_remote_copy(
        src_ref=src, dst_ref=dst, send_sem=send, recv_sem=recv, device_id=(p, q), device_id_type=MESH
    )


def fused(
    n_rows, n_cols, a_ref, l_ref, d_ref, y_ref, g_ref,
    l_buf, part, right_buf, left_buf, term, plane_buf, col_buf, gath,
    l_send, l_recv, r_send, r_recv, f_send, f_recv, p_send, p_recv, c_send, c_recv, g_send, g_recv,
):
    p = lax.axis_index("prow")
    q = lax.axis_index("pcol")
    nodes, ratio, block, width = l_buf.shape
    piece = block // n_cols
    seg = width // n_rows
    chunk = block // (2 * SUB)
    hi = p // n_cols
    lo = p % n_cols
    t = jnp.int32(0)
    bit = 1
    while bit < n_cols:
        t = t + bit * (((lo // bit) + (q // bit)) % 2)
        bit *= 2
    pair = p + 1 - 2 * (p % 2)

    def beside(j):
        lo2 = jnp.int32(0)
        b = 1
        while b < n_cols:
            lo2 = lo2 + b * (((lo // b) + (2 * j // b)) % 2)
            b *= 2
        return hi * n_cols + lo2

    barrier = pltpu.get_barrier_semaphore()
    for k in range(1, n_rows):
        pl.semaphore_signal(barrier, inc=1, device_id=((p + k) % n_rows, q), device_id_type=MESH)
    for k in range(1, n_cols):
        pl.semaphore_signal(barrier, inc=1, device_id=(p, (q + k) % n_cols), device_id_type=MESH)
    pl.semaphore_wait(barrier, n_rows + n_cols - 2)

    def rows(c):
        return pl.ds(pl.multiple_of(c * chunk, chunk), chunk)

    def l_slot(s, h, c):
        return l_buf.at[s, h, rows(c)]

    def to_peer_hi(s, c, k, src):
        return remote(src, l_slot(s, hi, c), l_send.at[s, c, k - 1], l_recv.at[s, hi, c],
                      (p + k * n_cols) % n_rows, q)

    def to_x(s, c, j, src):
        return remote(src, l_slot(s, hi, c), l_send.at[s, c, ratio - 1 + j - 1], l_recv.at[s, hi, c],
                      beside(j), q)

    def to_pair(s, c, k, src):
        h = (hi + k) % ratio
        return remote(src, l_slot(s, h, c), l_send.at[s, c, ratio - 1 + n_cols // 2 - 1 + k],
                      l_recv.at[s, h, c], pair, q)

    def l_arrived(s, c, h):
        remote(l_slot(s, h, c), l_slot(s, h, c), l_send.at[s, c, 0], l_recv.at[s, h, c], pair, q).wait_recv()

    owner = t == 0
    source_chip = t < 2
    core = p % 2

    def mine(u):
        return core * SUB + u

    def other(u):
        return (1 - core) * SUB + u

    @pl.when(owner)
    def _():
        for s in range(nodes):
            for u in range(SUB):
                to_pair(s, other(u), 0, l_ref.at[s, rows(other(u))]).start()
            for u in range(SUB):
                src = l_ref.at[s, rows(mine(u))]
                for j in range(1, n_cols // 2):
                    to_x(s, mine(u), j, src).start()
                for k in range(1, ratio):
                    to_peer_hi(s, mine(u), k, src).start()
            for u in range(SUB):
                to_pair(s, mine(u), 0, l_ref.at[s, rows(mine(u))]).start()
        for s in range(nodes):
            l_buf[s, hi] = l_ref[s]

    def receive_blocks(s):
        for u in range(SUB):
            c = mine(u)
            src = l_slot(s, hi, c)

            @pl.when(jnp.logical_not(owner))
            def _():
                l_arrived(s, c, hi)
                for k in range(1, ratio):
                    to_peer_hi(s, c, k, src).start()

            @pl.when(t == 1)
            def _():
                for j in range(1, n_cols // 2):
                    to_x(s, c, j, src).start()

            @pl.when(jnp.logical_not(source_chip))
            def _():
                to_pair(s, c, 0, src).start()

        for u in range(SUB):
            c = mine(u)
            for k in range(1, ratio):
                l_arrived(s, c, (hi + k) % ratio)
                to_pair(s, c, k, l_slot(s, (hi + k) % ratio, c)).start()
        for u in range(SUB):
            c = other(u)

            @pl.when(jnp.logical_not(owner))
            def _():
                l_arrived(s, c, hi)

            for k in range(1, ratio):
                l_arrived(s, c, (hi + k) % ratio)

    def drain_blocks(s):
        for u in range(SUB):
            c = mine(u)
            src = l_slot(s, hi, c)
            for k in range(1, ratio):
                to_peer_hi(s, c, k, src).wait_send()
                to_pair(s, c, k, src).wait_send()

            @pl.when(source_chip)
            def _():
                for j in range(1, n_cols // 2):
                    to_x(s, c, j, src).wait_send()

            @pl.when(t != 1)
            def _():
                to_pair(s, c, 0, src).wait_send()

            @pl.when(owner)
            def _():
                to_pair(s, other(u), 0, src).wait_send()

    def multiply(s):
        total = jnp.dot(a_ref[s, 0], l_buf[s, 0], preferred_element_type=jnp.float32)
        for h in range(1, ratio):
            total += jnp.dot(a_ref[s, h], l_buf[s, h], preferred_element_type=jnp.float32)
        for d in range(n_cols):
            part[s, d] = total[d * piece:(d + 1) * piece]
        return total

    def diagonal_term(s, total):
        high = total.astype(jnp.bfloat16)
        low = (total - high.astype(jnp.float32)).astype(jnp.bfloat16)
        over_rows = (((0,), (0,)), ((), ()))
        product = lax.dot_general(l_ref[s], high, over_rows, preferred_element_type=jnp.float32)
        product += lax.dot_general(l_ref[s], low, over_rows, preferred_element_type=jnp.float32)
        for k in range(n_rows):
            term[s, k] = product[k * seg:(k + 1) * seg]

    def right_copy(s, d, src):
        return remote(src, right_buf.at[s, d], r_send.at[s, d], r_recv.at[s, d], p, (q + 1) % n_cols)

    def left_copy(s, d, src):
        return remote(src, left_buf.at[s, d], f_send.at[s, d], f_recv.at[s, d], p, (q + n_cols - 1) % n_cols)

    def line_start(s, nearest):
        @pl.when(q == 0)
        def _():
            for d in ((1,) if nearest else range(n_cols - 1, 1, -1)):
                right_copy(s, d, part.at[s, d]).start()

        @pl.when(q == n_cols - 1)
        def _():
            for d in ((n_cols - 2,) if nearest else range(n_cols - 2)):
                left_copy(s, d, part.at[s, d]).start()

    def line_relay(s):
        for i in range(n_cols - 2):
            d = n_cols - 1 - i

            @pl.when(jnp.logical_and(q > 0, q < d))
            def _():
                right_copy(s, d, right_buf.at[s, d]).wait_recv()
                right_buf[s, d] = right_buf[s, d] + part[s, d]
                right_copy(s, d, right_buf.at[s, d]).start()

            e = i

            @pl.when(jnp.logical_and(q < n_cols - 1, q > e))
            def _():
                left_copy(s, e, left_buf.at[s, e]).wait_recv()
                left_buf[s, e] = left_buf[s, e] + part[s, e]
                left_copy(s, e, left_buf.at[s, e]).start()

    def line_finish(s):
        @pl.when(q > 0)
        def _():
            right_copy(s, q, right_buf.at[s, q]).wait_recv()
            part[s, q] = part[s, q] + right_buf[s, q]

        @pl.when(q < n_cols - 1)
        def _():
            left_copy(s, q, left_buf.at[s, q]).wait_recv()
            part[s, q] = part[s, q] + left_buf[s, q]

        y_ref[s] = (-part[s, q]).astype(jnp.bfloat16)

    def line_drain(s):
        for d in range(n_cols):
            @pl.when(q < d)
            def _():
                right_copy(s, d, part.at[s, d]).wait_send()

            @pl.when(q > d)
            def _():
                left_copy(s, d, part.at[s, d]).wait_send()

    def plane_copy(s, k):
        to = (p + k) % n_rows
        return remote(term.at[s, to], plane_buf.at[s, n_rows - k], p_send.at[s, k], p_recv.at[s, n_rows - k], to, q)

    def plane_wait(s, k):
        remote(term.at[s, 0], plane_buf.at[s, k], p_send.at[s, k], p_recv.at[s, k], pair, q).wait_recv()

    def col_copy(s, k):
        to = (q + k) % n_cols
        return remote(col_buf.at[s, q], col_buf.at[s, q], c_send.at[s, k], c_recv.at[s, n_cols - k], p, to)

    def col_wait(s, k):
        src = (q + k) % n_cols
        remote(col_buf.at[s, src], col_buf.at[s, src], c_send.at[s, k], c_recv.at[s, k], pair, q).wait_recv()

    def gath_copy(s, k):
        to = (p + k) % n_rows
        return remote(gath.at[s, p], gath.at[s, p], g_send.at[s, k], g_recv.at[s, n_rows - k], to, q)

    def gath_wait(s, k):
        src = (p + k) % n_rows
        remote(gath.at[s, src], gath.at[s, src], g_send.at[s, k], g_recv.at[s, k], pair, q).wait_recv()

    def plane_start(s):
        for k in range(1, n_rows):
            plane_copy(s, k).start()

    def col_start(s):
        total = term[s, p]
        for k in range(1, n_rows):
            plane_wait(s, k)
            total = total + plane_buf[s, k]
        col_buf[s, q] = total
        for k in range(1, n_cols):
            col_copy(s, k).start()

    def gath_start(s):
        for k in range(1, n_cols):
            col_wait(s, k)
        total = col_buf[s, 0]
        for k in range(1, n_cols):
            total = total + col_buf[s, k]
        gath[s, p] = d_ref[s, pl.ds(pl.multiple_of(p * seg, seg), seg)] + total
        for k in range(1, n_rows):
            gath_copy(s, k).start()

    for s in range(nodes):
        receive_blocks(s)
        total = multiply(s)
        if s > 0:
            col_start(s - 1)
            line_start(s - 1, True)
        line_start(s, False)
        diagonal_term(s, total)
        plane_start(s)
    for s in range(nodes):
        line_relay(s)
        if s == 0:
            col_start(nodes - 1)
            line_start(nodes - 1, True)
        if s < nodes - 1:
            gath_start(s)
    gath_start(nodes - 1)
    for s in range(nodes):
        line_finish(s)
    for s in range(nodes):
        drain_blocks(s)
        line_drain(s)
        for k in range(1, n_rows):
            plane_copy(s, k).wait_send()
        for k in range(1, n_cols):
            col_copy(s, k).wait_send()
    for s in range(nodes):
        for k in range(1, n_rows):
            gath_wait(s, k)
        for k in range(n_rows):
            g_ref[s, k * seg:(k + 1) * seg] = gath[s, k]
    for s in range(nodes):
        for k in range(1, n_rows):
            gath_copy(s, k).wait_send()


def pick(
    n_rows, n_cols, structure_ref, inverse_ref, panel_ref, a_ref, l_ref, mask_ref, raw, wide, a_sem, l_sem
):
    p = lax.axis_index("prow")
    q = lax.axis_index("pcol")
    nodes, ratio, block, _ = a_ref.shape
    _, strips, strip, cols_local, _ = raw.shape
    rows_local = inverse_ref.shape[0]
    listed = structure_ref.shape[1]

    def find(s, residue, divisor):
        found = jnp.int32(0)
        for i in range(listed):
            value = structure_ref[s, i]
            found = found + jnp.where(value % n_rows == residue, value // divisor, 0)
        return found

    copies = []
    for s in range(nodes):
        row = find(s, p, n_rows)
        factor = pltpu.make_async_copy(panel_ref.at[s, row], l_ref.at[s], l_sem.at[s])
        factor.start()
        copies.append(factor)
        for k in range(strips):
            pltpu.make_async_copy(
                inverse_ref.at[row, pl.ds(k * strip, strip)], raw.at[s, k], a_sem.at[s, k]
            ).start()
        for r in range(rows_local):
            mask_ref[s, r] = jnp.where(row == r, 1, 0).astype(jnp.int32)
    for s in range(nodes):
        cols = [find(s, h * n_cols + q, n_cols) for h in range(ratio)]
        for k in range(strips):
            pltpu.make_async_copy(
                inverse_ref.at[0, pl.ds(k * strip, strip)], raw.at[s, k], a_sem.at[s, k]
            ).wait()
            slot = k % 2
            for b in range(block // 128):
                lanes = raw[s, k, :, :, b * 128:(b + 1) * 128].astype(jnp.float32)
                wide[slot, b] = lanes.reshape(strip * cols_local, 128)
            for h in range(ratio):
                for b in range(block // 128):
                    a_ref[s, h, k * strip:(k + 1) * strip, b * 128:(b + 1) * 128] = wide[
                        slot, b, pl.ds(cols[h], strip, stride=cols_local)
                    ].astype(jnp.bfloat16)
    for factor in copies:
        factor.wait()


def on_device(inverse, panel, structure, diag_inverse):
    n_rows = lax.axis_size("prow")
    n_cols = lax.axis_size("pcol")
    rows_local, block, cols_local, _ = inverse.shape
    nodes, _, _, width = panel.shape
    ratio = n_rows // n_cols
    piece = block // n_cols
    seg = width // n_rows
    strip = block // STRIPS

    vmem = pl.BlockSpec(memory_space=pltpu.VMEM)
    smem = pl.BlockSpec(memory_space=pltpu.SMEM)
    hbm = pl.BlockSpec(memory_space=pltpu.HBM)
    a_sel, l_sel, mask = pl.pallas_call(
        functools.partial(pick, n_rows, n_cols),
        out_shape=(
            jax.ShapeDtypeStruct((nodes, ratio, block, block), jnp.bfloat16),
            jax.ShapeDtypeStruct((nodes, block, width), jnp.bfloat16),
            jax.ShapeDtypeStruct((nodes, rows_local), jnp.int32),
        ),
        in_specs=[smem, hbm, hbm],
        out_specs=(vmem, vmem, smem),
        scratch_shapes=[
            pltpu.VMEM((nodes, STRIPS, strip, cols_local, block), jnp.bfloat16),
            pltpu.VMEM((2, block // 128, strip * cols_local, 128), jnp.float32),
            pltpu.SemaphoreType.DMA((nodes, STRIPS)),
            pltpu.SemaphoreType.DMA((nodes,)),
        ],
        compiler_params=pltpu.CompilerParams(vmem_limit_bytes=50 * 1024 * 1024),
        name="pick_blocks",
    )(structure, inverse, panel)

    f32 = jnp.float32
    dma = pltpu.SemaphoreType.DMA
    sends = ratio - 1 + n_cols // 2 - 1 + ratio
    pieces, diagonal = pl.pallas_call(
        functools.partial(fused, n_rows, n_cols),
        out_shape=(
            jax.ShapeDtypeStruct((nodes, piece, width), jnp.bfloat16),
            jax.ShapeDtypeStruct((nodes, width, width), f32),
        ),
        in_specs=[vmem] * 3,
        out_specs=(vmem, vmem),
        scratch_shapes=[
            pltpu.VMEM((nodes, ratio, block, width), jnp.bfloat16),
            pltpu.VMEM((nodes, n_cols, piece, width), f32),
            pltpu.VMEM((nodes, n_cols, piece, width), f32),
            pltpu.VMEM((nodes, n_cols, piece, width), f32),
            pltpu.VMEM((nodes, n_rows, seg, width), f32),
            pltpu.VMEM((nodes, n_rows, seg, width), f32),
            pltpu.VMEM((nodes, n_cols, seg, width), f32),
            pltpu.VMEM((nodes, n_rows, seg, width), f32),
            dma((nodes, 2 * SUB, sends)), dma((nodes, ratio, 2 * SUB)),
            dma((nodes, n_cols)), dma((nodes, n_cols)),
            dma((nodes, n_cols)), dma((nodes, n_cols)),
            dma((nodes, n_rows)), dma((nodes, n_rows)),
            dma((nodes, n_cols)), dma((nodes, n_cols)),
            dma((nodes, n_rows)), dma((nodes, n_rows)),
        ],
        compiler_params=pltpu.CompilerParams(
            collective_id=0, has_side_effects=True, vmem_limit_bytes=40 * 1024 * 1024
        ),
        name="selected_inverse",
    )(a_sel, l_sel, diag_inverse)

    off_diag = jnp.where(mask[:, :, None, None] > 0, pieces[:, None], jnp.zeros((), jnp.bfloat16))
    return off_diag, diagonal


def solution(mesh):
    placed = (P(None, "prow", None, "pcol"), P(None, None, "prow", None), P(), P())
    return jax.shard_map(
        on_device,
        mesh=mesh,
        in_specs=placed,
        out_specs=(P(None, None, ("prow", "pcol"), None), P()),
        check_vma=False,
    )
```

```python
import functools

import jax
import jax.numpy as jnp
from jax import lax
from jax.experimental import pallas as pl
from jax.experimental.pallas import tpu as pltpu
from jax.sharding import PartitionSpec as P

MESH = pl.DeviceIdType.MESH
SUB = 2
STRIPS = 4


def remote(src, dst, send, recv, p, q):
    return pltpu.make_async_remote_copy(
        src_ref=src, dst_ref=dst, send_sem=send, recv_sem=recv, device_id=(p, q), device_id_type=MESH
    )


def fused(
    n_rows, n_cols, a_ref, l_ref, d_ref, y_ref, g_ref,
    l_buf, part, right_buf, left_buf, right_scale, left_scale, term, plane_buf, col_buf, gath,
    l_send, l_recv, r_send, r_recv, f_send, f_recv, p_send, p_recv, c_send, c_recv, g_send, g_recv,
):
    p = lax.axis_index("prow")
    q = lax.axis_index("pcol")
    nodes, ratio, block, width = l_buf.shape
    piece = block // n_cols
    seg = width // n_rows
    chunk = block // (2 * SUB)
    hi = p // n_cols
    lo = p % n_cols
    t = jnp.int32(0)
    bit = 1
    while bit < n_cols:
        t = t + bit * (((lo // bit) + (q // bit)) % 2)
        bit *= 2
    pair = p + 1 - 2 * (p % 2)

    def beside(j):
        lo2 = jnp.int32(0)
        b = 1
        while b < n_cols:
            lo2 = lo2 + b * (((lo // b) + (2 * j // b)) % 2)
            b *= 2
        return hi * n_cols + lo2

    barrier = pltpu.get_barrier_semaphore()
    for k in range(1, n_rows):
        pl.semaphore_signal(barrier, inc=1, device_id=((p + k) % n_rows, q), device_id_type=MESH)
    for k in range(1, n_cols):
        pl.semaphore_signal(barrier, inc=1, device_id=(p, (q + k) % n_cols), device_id_type=MESH)
    pl.semaphore_wait(barrier, n_rows + n_cols - 2)

    def rows(c):
        return pl.ds(pl.multiple_of(c * chunk, chunk), chunk)

    def l_slot(s, h, c):
        return l_buf.at[s, h, rows(c)]

    def to_peer_hi(s, c, k, src):
        return remote(src, l_slot(s, hi, c), l_send.at[s, c, k - 1], l_recv.at[s, hi, c],
                      (p + k * n_cols) % n_rows, q)

    def to_x(s, c, j, src):
        return remote(src, l_slot(s, hi, c), l_send.at[s, c, ratio - 1 + j - 1], l_recv.at[s, hi, c],
                      beside(j), q)

    def to_pair(s, c, k, src):
        h = (hi + k) % ratio
        return remote(src, l_slot(s, h, c), l_send.at[s, c, ratio - 1 + n_cols // 2 - 1 + k],
                      l_recv.at[s, h, c], pair, q)

    def l_arrived(s, c, h):
        remote(l_slot(s, h, c), l_slot(s, h, c), l_send.at[s, c, 0], l_recv.at[s, h, c], pair, q).wait_recv()

    owner = t == 0
    source_chip = t < 2
    core = p % 2

    def mine(u):
        return core * SUB + u

    def other(u):
        return (1 - core) * SUB + u

    @pl.when(owner)
    def _():
        for s in range(nodes):
            for u in range(SUB):
                to_pair(s, other(u), 0, l_ref.at[s, rows(other(u))]).start()
            for u in range(SUB):
                src = l_ref.at[s, rows(mine(u))]
                for j in range(1, n_cols // 2):
                    to_x(s, mine(u), j, src).start()
                for k in range(1, ratio):
                    to_peer_hi(s, mine(u), k, src).start()
            for u in range(SUB):
                to_pair(s, mine(u), 0, l_ref.at[s, rows(mine(u))]).start()
        for s in range(nodes):
            l_buf[s, hi] = l_ref[s]

    def receive_blocks(s):
        for u in range(SUB):
            c = mine(u)
            src = l_slot(s, hi, c)

            @pl.when(jnp.logical_not(owner))
            def _():
                l_arrived(s, c, hi)
                for k in range(1, ratio):
                    to_peer_hi(s, c, k, src).start()

            @pl.when(t == 1)
            def _():
                for j in range(1, n_cols // 2):
                    to_x(s, c, j, src).start()

            @pl.when(jnp.logical_not(source_chip))
            def _():
                to_pair(s, c, 0, src).start()

        for u in range(SUB):
            c = mine(u)
            for k in range(1, ratio):
                l_arrived(s, c, (hi + k) % ratio)
                to_pair(s, c, k, l_slot(s, (hi + k) % ratio, c)).start()
        for u in range(SUB):
            c = other(u)

            @pl.when(jnp.logical_not(owner))
            def _():
                l_arrived(s, c, hi)

            for k in range(1, ratio):
                l_arrived(s, c, (hi + k) % ratio)

    def drain_blocks(s):
        for u in range(SUB):
            c = mine(u)
            src = l_slot(s, hi, c)
            for k in range(1, ratio):
                to_peer_hi(s, c, k, src).wait_send()
                to_pair(s, c, k, src).wait_send()

            @pl.when(source_chip)
            def _():
                for j in range(1, n_cols // 2):
                    to_x(s, c, j, src).wait_send()

            @pl.when(t != 1)
            def _():
                to_pair(s, c, 0, src).wait_send()

            @pl.when(owner)
            def _():
                to_pair(s, other(u), 0, src).wait_send()

    def multiply(s):
        total = jnp.dot(a_ref[s, 0], l_buf[s, 0], preferred_element_type=jnp.float32)
        for h in range(1, ratio):
            total += jnp.dot(a_ref[s, h], l_buf[s, h], preferred_element_type=jnp.float32)
        for d in range(n_cols):
            part[s, d] = total[d * piece:(d + 1) * piece]
        return total

    def diagonal_term(s, total):
        high = total.astype(jnp.bfloat16)
        low = (total - high.astype(jnp.float32)).astype(jnp.bfloat16)
        over_rows = (((0,), (0,)), ((), ()))
        product = lax.dot_general(l_ref[s], high, over_rows, preferred_element_type=jnp.float32)
        product += lax.dot_general(l_ref[s], low, over_rows, preferred_element_type=jnp.float32)
        for k in range(n_rows):
            term[s, k] = product[k * seg:(k + 1) * seg]

    def encode(s, d, value, buf, scale):
        largest = jnp.maximum(jnp.max(jnp.abs(value), axis=0, keepdims=True), 1e-30)
        buf[s, d] = jnp.floor(value * (32700.0 / largest) + 0.5).astype(jnp.int32).astype(jnp.int16)
        scale[s, d] = jnp.broadcast_to(largest * (1.0 / 32700.0), scale.shape[2:])

    def decode(s, d, buf, scale):
        return buf[s, d].astype(jnp.int32).astype(jnp.float32) * scale[s, d][0:1]

    class line_copy:
        def __init__(self, s, d, buf, scale, send, recv, to):
            self.copies = [
                remote(buf.at[s, d], buf.at[s, d], send.at[0, s, d], recv.at[0, s, d], p, to),
                remote(scale.at[s, d], scale.at[s, d], send.at[1, s, d], recv.at[1, s, d], p, to),
            ]

        def start(self):
            for copy in self.copies:
                copy.start()

        def wait_send(self):
            for copy in self.copies:
                copy.wait_send()

        def wait_recv(self):
            for copy in self.copies:
                copy.wait_recv()

    def right_copy(s, d):
        return line_copy(s, d, right_buf, right_scale, r_send, r_recv, (q + 1) % n_cols)

    def left_copy(s, d):
        return line_copy(s, d, left_buf, left_scale, f_send, f_recv, (q + n_cols - 1) % n_cols)

    def line_start(s, nearest):
        @pl.when(q == 0)
        def _():
            for d in ((1,) if nearest else range(n_cols - 1, 1, -1)):
                encode(s, d, part[s, d], right_buf, right_scale)
                right_copy(s, d).start()

        @pl.when(q == n_cols - 1)
        def _():
            for d in ((n_cols - 2,) if nearest else range(n_cols - 2)):
                encode(s, d, part[s, d], left_buf, left_scale)
                left_copy(s, d).start()

    def line_relay(s):
        for i in range(n_cols - 2):
            d = n_cols - 1 - i

            @pl.when(jnp.logical_and(q > 0, q < d))
            def _():
                right_copy(s, d).wait_recv()
                encode(s, d, decode(s, d, right_buf, right_scale) + part[s, d], right_buf, right_scale)
                right_copy(s, d).start()

            e = i

            @pl.when(jnp.logical_and(q < n_cols - 1, q > e))
            def _():
                left_copy(s, e).wait_recv()
                encode(s, e, decode(s, e, left_buf, left_scale) + part[s, e], left_buf, left_scale)
                left_copy(s, e).start()

    def line_finish(s):
        @pl.when(q > 0)
        def _():
            right_copy(s, q).wait_recv()
            part[s, q] = part[s, q] + decode(s, q, right_buf, right_scale)

        @pl.when(q < n_cols - 1)
        def _():
            left_copy(s, q).wait_recv()
            part[s, q] = part[s, q] + decode(s, q, left_buf, left_scale)

        y_ref[s] = (-part[s, q]).astype(jnp.bfloat16)

    def line_drain(s):
        for d in range(n_cols):
            @pl.when(q < d)
            def _():
                right_copy(s, d).wait_send()

            @pl.when(q > d)
            def _():
                left_copy(s, d).wait_send()

    def plane_copy(s, k):
        to = (p + k) % n_rows
        return remote(term.at[s, to], plane_buf.at[s, n_rows - k], p_send.at[s, k], p_recv.at[s, n_rows - k], to, q)

    def plane_wait(s, k):
        remote(term.at[s, 0], plane_buf.at[s, k], p_send.at[s, k], p_recv.at[s, k], pair, q).wait_recv()

    def col_copy(s, k):
        to = (q + k) % n_cols
        return remote(col_buf.at[s, q], col_buf.at[s, q], c_send.at[s, k], c_recv.at[s, n_cols - k], p, to)

    def col_wait(s, k):
        src = (q + k) % n_cols
        remote(col_buf.at[s, src], col_buf.at[s, src], c_send.at[s, k], c_recv.at[s, k], pair, q).wait_recv()

    def gath_copy(s, k):
        to = (p + k) % n_rows
        return remote(gath.at[s, p], gath.at[s, p], g_send.at[s, k], g_recv.at[s, n_rows - k], to, q)

    def gath_wait(s, k):
        src = (p + k) % n_rows
        remote(gath.at[s, src], gath.at[s, src], g_send.at[s, k], g_recv.at[s, k], pair, q).wait_recv()

    def plane_start(s):
        for k in range(1, n_rows):
            plane_copy(s, k).start()

    def col_start(s):
        total = term[s, p]
        for k in range(1, n_rows):
            plane_wait(s, k)
            total = total + plane_buf[s, k]
        col_buf[s, q] = total
        for k in range(1, n_cols):
            col_copy(s, k).start()

    def gath_start(s):
        for k in range(1, n_cols):
            col_wait(s, k)
        total = col_buf[s, 0]
        for k in range(1, n_cols):
            total = total + col_buf[s, k]
        gath[s, p] = d_ref[s, pl.ds(pl.multiple_of(p * seg, seg), seg)] + total
        for k in range(1, n_rows):
            gath_copy(s, k).start()

    for s in range(nodes):
        receive_blocks(s)
        total = multiply(s)
        if s > 0:
            col_start(s - 1)
            line_start(s - 1, True)
        line_start(s, False)
        diagonal_term(s, total)
        plane_start(s)
    for s in range(nodes):
        line_relay(s)
        if s == 0:
            col_start(nodes - 1)
            line_start(nodes - 1, True)
        if s < nodes - 1:
            gath_start(s)
    gath_start(nodes - 1)
    for s in range(nodes):
        line_finish(s)
    for s in range(nodes):
        drain_blocks(s)
        line_drain(s)
        for k in range(1, n_rows):
            plane_copy(s, k).wait_send()
        for k in range(1, n_cols):
            col_copy(s, k).wait_send()
    for s in range(nodes):
        for k in range(1, n_rows):
            gath_wait(s, k)
        for k in range(n_rows):
            g_ref[s, k * seg:(k + 1) * seg] = gath[s, k]
    for s in range(nodes):
        for k in range(1, n_rows):
            gath_copy(s, k).wait_send()


def pick(
    n_rows, n_cols, structure_ref, inverse_ref, panel_ref, a_ref, l_ref, mask_ref, raw, wide, a_sem, l_sem
):
    p = lax.axis_index("prow")
    q = lax.axis_index("pcol")
    nodes, ratio, block, _ = a_ref.shape
    _, strips, strip, cols_local, _ = raw.shape
    rows_local = inverse_ref.shape[0]
    listed = structure_ref.shape[1]

    def find(s, residue, divisor):
        found = jnp.int32(0)
        for i in range(listed):
            value = structure_ref[s, i]
            found = found + jnp.where(value % n_rows == residue, value // divisor, 0)
        return found

    copies = []
    for s in range(nodes):
        row = find(s, p, n_rows)
        factor = pltpu.make_async_copy(panel_ref.at[s, row], l_ref.at[s], l_sem.at[s])
        factor.start()
        copies.append(factor)
        for k in range(strips):
            pltpu.make_async_copy(
                inverse_ref.at[row, pl.ds(k * strip, strip)], raw.at[s, k], a_sem.at[s, k]
            ).start()
        for r in range(rows_local):
            mask_ref[s, r] = jnp.where(row == r, 1, 0).astype(jnp.int32)
    for s in range(nodes):
        cols = [find(s, h * n_cols + q, n_cols) for h in range(ratio)]
        for k in range(strips):
            pltpu.make_async_copy(
                inverse_ref.at[0, pl.ds(k * strip, strip)], raw.at[s, k], a_sem.at[s, k]
            ).wait()
            slot = k % 2
            for b in range(block // 128):
                lanes = raw[s, k, :, :, b * 128:(b + 1) * 128].astype(jnp.float32)
                wide[slot, b] = lanes.reshape(strip * cols_local, 128)
            for h in range(ratio):
                for b in range(block // 128):
                    a_ref[s, h, k * strip:(k + 1) * strip, b * 128:(b + 1) * 128] = wide[
                        slot, b, pl.ds(cols[h], strip, stride=cols_local)
                    ].astype(jnp.bfloat16)
    for factor in copies:
        factor.wait()


def on_device(inverse, panel, structure, diag_inverse):
    n_rows = lax.axis_size("prow")
    n_cols = lax.axis_size("pcol")
    rows_local, block, cols_local, _ = inverse.shape
    nodes, _, _, width = panel.shape
    ratio = n_rows // n_cols
    piece = block // n_cols
    seg = width // n_rows
    strip = block // STRIPS

    vmem = pl.BlockSpec(memory_space=pltpu.VMEM)
    smem = pl.BlockSpec(memory_space=pltpu.SMEM)
    hbm = pl.BlockSpec(memory_space=pltpu.HBM)
    a_sel, l_sel, mask = pl.pallas_call(
        functools.partial(pick, n_rows, n_cols),
        out_shape=(
            jax.ShapeDtypeStruct((nodes, ratio, block, block), jnp.bfloat16),
            jax.ShapeDtypeStruct((nodes, block, width), jnp.bfloat16),
            jax.ShapeDtypeStruct((nodes, rows_local), jnp.int32),
        ),
        in_specs=[smem, hbm, hbm],
        out_specs=(vmem, vmem, smem),
        scratch_shapes=[
            pltpu.VMEM((nodes, STRIPS, strip, cols_local, block), jnp.bfloat16),
            pltpu.VMEM((2, block // 128, strip * cols_local, 128), jnp.float32),
            pltpu.SemaphoreType.DMA((nodes, STRIPS)),
            pltpu.SemaphoreType.DMA((nodes,)),
        ],
        compiler_params=pltpu.CompilerParams(vmem_limit_bytes=50 * 1024 * 1024),
        name="pick_blocks",
    )(structure, inverse, panel)

    f32 = jnp.float32
    dma = pltpu.SemaphoreType.DMA
    sends = ratio - 1 + n_cols // 2 - 1 + ratio
    pieces, diagonal = pl.pallas_call(
        functools.partial(fused, n_rows, n_cols),
        out_shape=(
            jax.ShapeDtypeStruct((nodes, piece, width), jnp.bfloat16),
            jax.ShapeDtypeStruct((nodes, width, width), f32),
        ),
        in_specs=[vmem] * 3,
        out_specs=(vmem, vmem),
        scratch_shapes=[
            pltpu.VMEM((nodes, ratio, block, width), jnp.bfloat16),
            pltpu.VMEM((nodes, n_cols, piece, width), f32),
            pltpu.VMEM((nodes, n_cols, piece, width), jnp.int16),
            pltpu.VMEM((nodes, n_cols, piece, width), jnp.int16),
            pltpu.VMEM((nodes, n_cols, 8, width), f32),
            pltpu.VMEM((nodes, n_cols, 8, width), f32),
            pltpu.VMEM((nodes, n_rows, seg, width), f32),
            pltpu.VMEM((nodes, n_rows, seg, width), f32),
            pltpu.VMEM((nodes, n_cols, seg, width), f32),
            pltpu.VMEM((nodes, n_rows, seg, width), f32),
            dma((nodes, 2 * SUB, sends)), dma((nodes, ratio, 2 * SUB)),
            dma((2, nodes, n_cols)), dma((2, nodes, n_cols)),
            dma((2, nodes, n_cols)), dma((2, nodes, n_cols)),
            dma((nodes, n_rows)), dma((nodes, n_rows)),
            dma((nodes, n_cols)), dma((nodes, n_cols)),
            dma((nodes, n_rows)), dma((nodes, n_rows)),
        ],
        compiler_params=pltpu.CompilerParams(
            collective_id=0, has_side_effects=True, vmem_limit_bytes=40 * 1024 * 1024
        ),
        name="selected_inverse",
    )(a_sel, l_sel, diag_inverse)

    off_diag = jnp.where(mask[:, :, None, None] > 0, pieces[:, None], jnp.zeros((), jnp.bfloat16))
    return off_diag, diagonal


def solution(mesh):
    placed = (P(None, "prow", None, "pcol"), P(None, None, "prow", None), P(), P())
    return jax.shard_map(
        on_device,
        mesh=mesh,
        in_specs=placed,
        out_specs=(P(None, None, ("prow", "pcol"), None), P()),
        check_vma=False,
    )
```

```python
import functools

import jax
import jax.numpy as jnp
from jax import lax
from jax.experimental import pallas as pl
from jax.experimental.pallas import tpu as pltpu
from jax.sharding import PartitionSpec as P

MESH = pl.DeviceIdType.MESH
SUB = 2
STRIPS = 4


def remote(src, dst, send, recv, p, q):
    return pltpu.make_async_remote_copy(
        src_ref=src, dst_ref=dst, send_sem=send, recv_sem=recv, device_id=(p, q), device_id_type=MESH
    )


def fused(
    n_rows, n_cols, a_ref, l_ref, d_ref, y_ref, g_ref,
    l_buf, part, right_buf, left_buf, right_scale, left_scale, term, plane_buf, col_buf, gath,
    l_send, l_recv, r_send, r_recv, f_send, f_recv, p_send, p_recv, c_send, c_recv, g_send, g_recv,
):
    p = lax.axis_index("prow")
    q = lax.axis_index("pcol")
    nodes, ratio, block, width = l_buf.shape
    piece = block // n_cols
    seg = width // n_rows
    chunk = block // (2 * SUB)
    hi = p // n_cols
    lo = p % n_cols
    t = jnp.int32(0)
    bit = 1
    while bit < n_cols:
        t = t + bit * (((lo // bit) + (q // bit)) % 2)
        bit *= 2
    pair = p + 1 - 2 * (p % 2)

    def beside(j):
        lo2 = jnp.int32(0)
        b = 1
        while b < n_cols:
            lo2 = lo2 + b * (((lo // b) + (2 * j // b)) % 2)
            b *= 2
        return hi * n_cols + lo2

    barrier = pltpu.get_barrier_semaphore()
    for k in range(1, n_rows):
        pl.semaphore_signal(barrier, inc=1, device_id=((p + k) % n_rows, q), device_id_type=MESH)
    for k in range(1, n_cols):
        pl.semaphore_signal(barrier, inc=1, device_id=(p, (q + k) % n_cols), device_id_type=MESH)
    pl.semaphore_wait(barrier, n_rows + n_cols - 2)

    def rows(c):
        return pl.ds(pl.multiple_of(c * chunk, chunk), chunk)

    def l_slot(s, h, c):
        return l_buf.at[s, h, rows(c)]

    def to_peer_hi(s, c, k, src):
        return remote(src, l_slot(s, hi, c), l_send.at[s, c, k - 1], l_recv.at[s, hi, c],
                      (p + k * n_cols) % n_rows, q)

    def to_x(s, c, j, src):
        return remote(src, l_slot(s, hi, c), l_send.at[s, c, ratio - 1 + j - 1], l_recv.at[s, hi, c],
                      beside(j), q)

    def to_pair(s, c, k, src):
        h = (hi + k) % ratio
        return remote(src, l_slot(s, h, c), l_send.at[s, c, ratio - 1 + n_cols // 2 - 1 + k],
                      l_recv.at[s, h, c], pair, q)

    def l_arrived(s, c, h):
        remote(l_slot(s, h, c), l_slot(s, h, c), l_send.at[s, c, 0], l_recv.at[s, h, c], pair, q).wait_recv()

    owner = t == 0
    source_chip = t < 2
    core = p % 2

    def mine(u):
        return core * SUB + u

    def other(u):
        return (1 - core) * SUB + u

    @pl.when(owner)
    def _():
        for s in range(nodes):
            for u in range(SUB):
                to_pair(s, other(u), 0, l_ref.at[s, rows(other(u))]).start()
            for u in range(SUB):
                src = l_ref.at[s, rows(mine(u))]
                for j in range(1, n_cols // 2):
                    to_x(s, mine(u), j, src).start()
                for k in range(1, ratio):
                    to_peer_hi(s, mine(u), k, src).start()
            for u in range(SUB):
                to_pair(s, mine(u), 0, l_ref.at[s, rows(mine(u))]).start()
        for s in range(nodes):
            l_buf[s, hi] = l_ref[s]

    def receive_blocks(s):
        for u in range(SUB):
            c = mine(u)
            src = l_slot(s, hi, c)

            @pl.when(jnp.logical_not(owner))
            def _():
                l_arrived(s, c, hi)
                for k in range(1, ratio):
                    to_peer_hi(s, c, k, src).start()

            @pl.when(t == 1)
            def _():
                for j in range(1, n_cols // 2):
                    to_x(s, c, j, src).start()

            @pl.when(jnp.logical_not(source_chip))
            def _():
                to_pair(s, c, 0, src).start()

        for u in range(SUB):
            c = mine(u)
            for k in range(1, ratio):
                l_arrived(s, c, (hi + k) % ratio)
                to_pair(s, c, k, l_slot(s, (hi + k) % ratio, c)).start()
        for u in range(SUB):
            c = other(u)

            @pl.when(jnp.logical_not(owner))
            def _():
                l_arrived(s, c, hi)

            for k in range(1, ratio):
                l_arrived(s, c, (hi + k) % ratio)

    def drain_blocks(s):
        for u in range(SUB):
            c = mine(u)
            src = l_slot(s, hi, c)
            for k in range(1, ratio):
                to_peer_hi(s, c, k, src).wait_send()
                to_pair(s, c, k, src).wait_send()

            @pl.when(source_chip)
            def _():
                for j in range(1, n_cols // 2):
                    to_x(s, c, j, src).wait_send()

            @pl.when(t != 1)
            def _():
                to_pair(s, c, 0, src).wait_send()

            @pl.when(owner)
            def _():
                to_pair(s, other(u), 0, src).wait_send()

    def multiply(s):
        total = jnp.dot(a_ref[s, 0], l_buf[s, 0], preferred_element_type=jnp.float32)
        for h in range(1, ratio):
            total += jnp.dot(a_ref[s, h], l_buf[s, h], preferred_element_type=jnp.float32)
        for d in range(n_cols):
            part[s, d] = total[d * piece:(d + 1) * piece]
        return total

    def diagonal_term(s, total):
        high = total.astype(jnp.bfloat16)
        low = (total - high.astype(jnp.float32)).astype(jnp.bfloat16)
        over_rows = (((0,), (0,)), ((), ()))
        product = lax.dot_general(l_ref[s], high, over_rows, preferred_element_type=jnp.float32)
        product += lax.dot_general(l_ref[s], low, over_rows, preferred_element_type=jnp.float32)
        for k in range(n_rows):
            term[s, k] = product[k * seg:(k + 1) * seg]

    def encode(s, d, value, buf, scale):
        largest = jnp.maximum(jnp.max(jnp.abs(value), axis=0, keepdims=True), 1e-30)
        buf[s, d] = jnp.floor(value * (32700.0 / largest) + 0.5).astype(jnp.int32).astype(jnp.int16)
        scale[s, d] = jnp.broadcast_to(largest * (1.0 / 32700.0), scale.shape[2:])

    def decode(s, d, buf, scale):
        return buf[s, d].astype(jnp.int32).astype(jnp.float32) * scale[s, d][0:1]

    class line_copy:
        def __init__(self, s, d, buf, scale, send, recv, to):
            self.copies = [
                remote(buf.at[s, d], buf.at[s, d], send.at[0, s, d], recv.at[0, s, d], p, to),
                remote(scale.at[s, d], scale.at[s, d], send.at[1, s, d], recv.at[1, s, d], p, to),
            ]

        def start(self):
            for copy in self.copies:
                copy.start()

        def wait_send(self):
            for copy in self.copies:
                copy.wait_send()

        def wait_recv(self):
            for copy in self.copies:
                copy.wait_recv()

    def right_copy(s, d):
        return line_copy(s, d, right_buf, right_scale, r_send, r_recv, (q + 1) % n_cols)

    def left_copy(s, d):
        return line_copy(s, d, left_buf, left_scale, f_send, f_recv, (q + n_cols - 1) % n_cols)

    def line_start(s, nearest):
        @pl.when(q == 0)
        def _():
            for d in ((1,) if nearest else range(n_cols - 1, 1, -1)):
                encode(s, d, part[s, d], right_buf, right_scale)
                right_copy(s, d).start()

        @pl.when(q == n_cols - 1)
        def _():
            for d in ((n_cols - 2,) if nearest else range(n_cols - 2)):
                encode(s, d, part[s, d], left_buf, left_scale)
                left_copy(s, d).start()

    def line_relay(s):
        for i in range(n_cols - 2):
            d = n_cols - 1 - i

            @pl.when(jnp.logical_and(q > 0, q < d))
            def _():
                right_copy(s, d).wait_recv()
                encode(s, d, decode(s, d, right_buf, right_scale) + part[s, d], right_buf, right_scale)
                right_copy(s, d).start()

            e = i

            @pl.when(jnp.logical_and(q < n_cols - 1, q > e))
            def _():
                left_copy(s, e).wait_recv()
                encode(s, e, decode(s, e, left_buf, left_scale) + part[s, e], left_buf, left_scale)
                left_copy(s, e).start()

    def line_finish(s):
        @pl.when(q > 0)
        def _():
            right_copy(s, q).wait_recv()
            part[s, q] = part[s, q] + decode(s, q, right_buf, right_scale)

        @pl.when(q < n_cols - 1)
        def _():
            left_copy(s, q).wait_recv()
            part[s, q] = part[s, q] + decode(s, q, left_buf, left_scale)

        y_ref[s] = (-part[s, q]).astype(jnp.bfloat16)

    def line_drain(s):
        for d in range(n_cols):
            @pl.when(q < d)
            def _():
                right_copy(s, d).wait_send()

            @pl.when(q > d)
            def _():
                left_copy(s, d).wait_send()

    def plane_copy(s, k):
        to = (p + k) % n_rows
        return remote(term.at[s, to], plane_buf.at[s, n_rows - k], p_send.at[s, k], p_recv.at[s, n_rows - k], to, q)

    def plane_wait(s, k):
        remote(term.at[s, 0], plane_buf.at[s, k], p_send.at[s, k], p_recv.at[s, k], pair, q).wait_recv()

    def col_copy(s, k):
        to = (q + k) % n_cols
        return remote(col_buf.at[s, q], col_buf.at[s, q], c_send.at[s, k], c_recv.at[s, n_cols - k], p, to)

    def col_wait(s, k):
        src = (q + k) % n_cols
        remote(col_buf.at[s, src], col_buf.at[s, src], c_send.at[s, k], c_recv.at[s, k], pair, q).wait_recv()

    def gath_copy(s, k):
        to = (p + k) % n_rows
        return remote(gath.at[s, p], gath.at[s, p], g_send.at[s, k], g_recv.at[s, n_rows - k], to, q)

    def gath_wait(s, k):
        src = (p + k) % n_rows
        remote(gath.at[s, src], gath.at[s, src], g_send.at[s, k], g_recv.at[s, k], pair, q).wait_recv()

    def plane_start(s):
        for k in range(1, n_rows):
            plane_copy(s, k).start()

    def col_start(s):
        total = term[s, p]
        for k in range(1, n_rows):
            plane_wait(s, k)
            total = total + plane_buf[s, k]
        col_buf[s, q] = total
        for k in range(1, n_cols):
            col_copy(s, k).start()

    def gath_start(s):
        for k in range(1, n_cols):
            col_wait(s, k)
        total = col_buf[s, 0]
        for k in range(1, n_cols):
            total = total + col_buf[s, k]
        gath[s, p] = d_ref[s, pl.ds(pl.multiple_of(p * seg, seg), seg)] + total
        for k in range(1, n_rows):
            gath_copy(s, k).start()

    for s in range(nodes):
        receive_blocks(s)
        total = multiply(s)
        diagonal_term(s, total)
        plane_start(s)
        if s > 0:
            col_start(s - 1)
            line_start(s - 1, True)
        line_start(s, False)
    for s in range(nodes):
        line_relay(s)
        if s == 0:
            col_start(nodes - 1)
            line_start(nodes - 1, True)
        if s < nodes - 1:
            gath_start(s)
    gath_start(nodes - 1)
    for s in range(nodes):
        line_finish(s)
    for s in range(nodes):
        drain_blocks(s)
        line_drain(s)
        for k in range(1, n_rows):
            plane_copy(s, k).wait_send()
        for k in range(1, n_cols):
            col_copy(s, k).wait_send()
    for s in range(nodes):
        for k in range(1, n_rows):
            gath_wait(s, k)
        for k in range(n_rows):
            g_ref[s, k * seg:(k + 1) * seg] = gath[s, k]
    for s in range(nodes):
        for k in range(1, n_rows):
            gath_copy(s, k).wait_send()


def pick(
    n_rows, n_cols, structure_ref, inverse_ref, panel_ref, a_ref, l_ref, mask_ref, raw, wide, a_sem, l_sem
):
    p = lax.axis_index("prow")
    q = lax.axis_index("pcol")
    nodes, ratio, block, _ = a_ref.shape
    _, strips, strip, cols_local, _ = raw.shape
    rows_local = inverse_ref.shape[0]
    listed = structure_ref.shape[1]

    def find(s, residue, divisor):
        found = jnp.int32(0)
        for i in range(listed):
            value = structure_ref[s, i]
            found = found + jnp.where(value % n_rows == residue, value // divisor, 0)
        return found

    copies = []
    for s in range(nodes):
        row = find(s, p, n_rows)
        factor = pltpu.make_async_copy(panel_ref.at[s, row], l_ref.at[s], l_sem.at[s])
        factor.start()
        copies.append(factor)
        for k in range(strips):
            pltpu.make_async_copy(
                inverse_ref.at[row, pl.ds(k * strip, strip)], raw.at[s, k], a_sem.at[s, k]
            ).start()
        for r in range(rows_local):
            mask_ref[s, r] = jnp.where(row == r, 1, 0).astype(jnp.int32)
    for s in range(nodes):
        cols = [find(s, h * n_cols + q, n_cols) for h in range(ratio)]
        for k in range(strips):
            pltpu.make_async_copy(
                inverse_ref.at[0, pl.ds(k * strip, strip)], raw.at[s, k], a_sem.at[s, k]
            ).wait()
            slot = k % 2
            for b in range(block // 128):
                lanes = raw[s, k, :, :, b * 128:(b + 1) * 128].astype(jnp.float32)
                wide[slot, b] = lanes.reshape(strip * cols_local, 128)
            for h in range(ratio):
                for b in range(block // 128):
                    a_ref[s, h, k * strip:(k + 1) * strip, b * 128:(b + 1) * 128] = wide[
                        slot, b, pl.ds(cols[h], strip, stride=cols_local)
                    ].astype(jnp.bfloat16)
    for factor in copies:
        factor.wait()


def on_device(inverse, panel, structure, diag_inverse):
    n_rows = lax.axis_size("prow")
    n_cols = lax.axis_size("pcol")
    rows_local, block, cols_local, _ = inverse.shape
    nodes, _, _, width = panel.shape
    ratio = n_rows // n_cols
    piece = block // n_cols
    seg = width // n_rows
    strip = block // STRIPS

    vmem = pl.BlockSpec(memory_space=pltpu.VMEM)
    smem = pl.BlockSpec(memory_space=pltpu.SMEM)
    hbm = pl.BlockSpec(memory_space=pltpu.HBM)
    a_sel, l_sel, mask = pl.pallas_call(
        functools.partial(pick, n_rows, n_cols),
        out_shape=(
            jax.ShapeDtypeStruct((nodes, ratio, block, block), jnp.bfloat16),
            jax.ShapeDtypeStruct((nodes, block, width), jnp.bfloat16),
            jax.ShapeDtypeStruct((nodes, rows_local), jnp.int32),
        ),
        in_specs=[smem, hbm, hbm],
        out_specs=(vmem, vmem, smem),
        scratch_shapes=[
            pltpu.VMEM((nodes, STRIPS, strip, cols_local, block), jnp.bfloat16),
            pltpu.VMEM((2, block // 128, strip * cols_local, 128), jnp.float32),
            pltpu.SemaphoreType.DMA((nodes, STRIPS)),
            pltpu.SemaphoreType.DMA((nodes,)),
        ],
        compiler_params=pltpu.CompilerParams(vmem_limit_bytes=50 * 1024 * 1024),
        name="pick_blocks",
    )(structure, inverse, panel)

    f32 = jnp.float32
    dma = pltpu.SemaphoreType.DMA
    sends = ratio - 1 + n_cols // 2 - 1 + ratio
    pieces, diagonal = pl.pallas_call(
        functools.partial(fused, n_rows, n_cols),
        out_shape=(
            jax.ShapeDtypeStruct((nodes, piece, width), jnp.bfloat16),
            jax.ShapeDtypeStruct((nodes, width, width), f32),
        ),
        in_specs=[vmem] * 3,
        out_specs=(vmem, vmem),
        scratch_shapes=[
            pltpu.VMEM((nodes, ratio, block, width), jnp.bfloat16),
            pltpu.VMEM((nodes, n_cols, piece, width), f32),
            pltpu.VMEM((nodes, n_cols, piece, width), jnp.int16),
            pltpu.VMEM((nodes, n_cols, piece, width), jnp.int16),
            pltpu.VMEM((nodes, n_cols, 8, width), f32),
            pltpu.VMEM((nodes, n_cols, 8, width), f32),
            pltpu.VMEM((nodes, n_rows, seg, width), f32),
            pltpu.VMEM((nodes, n_rows, seg, width), f32),
            pltpu.VMEM((nodes, n_cols, seg, width), f32),
            pltpu.VMEM((nodes, n_rows, seg, width), f32),
            dma((nodes, 2 * SUB, sends)), dma((nodes, ratio, 2 * SUB)),
            dma((2, nodes, n_cols)), dma((2, nodes, n_cols)),
            dma((2, nodes, n_cols)), dma((2, nodes, n_cols)),
            dma((nodes, n_rows)), dma((nodes, n_rows)),
            dma((nodes, n_cols)), dma((nodes, n_cols)),
            dma((nodes, n_rows)), dma((nodes, n_rows)),
        ],
        compiler_params=pltpu.CompilerParams(
            collective_id=0, has_side_effects=True, vmem_limit_bytes=40 * 1024 * 1024
        ),
        name="selected_inverse",
    )(a_sel, l_sel, diag_inverse)

    off_diag = jnp.where(mask[:, :, None, None] > 0, pieces[:, None], jnp.zeros((), jnp.bfloat16))
    return off_diag, diagonal


def solution(mesh):
    placed = (P(None, "prow", None, "pcol"), P(None, None, "prow", None), P(), P())
    return jax.shard_map(
        on_device,
        mesh=mesh,
        in_specs=placed,
        out_specs=(P(None, None, ("prow", "pcol"), None), P()),
        check_vma=False,
    )
```
